32 devices in a mesh: tm: 8 (over z, core), sec: 4 (over y, x).
Axes of the slice: x: 2, y: 2, z: 4, core: 2. Of those that a mesh axis runs over, the one named last changes fastest.
Arguments:
- green_occ: float32 [8, 4, 512, 512], P('tm', 'sec'), may hold values from -6 to 6
- virtual_green_time: float32 [8, 4, 512, 512], P('tm', 'sec'), may hold values from -6 to 6
- fit_rows: int32 [4, 12], P('sec'), may hold values from 0 to 5, as said below
- fit_cols: int32 [4, 12], P('sec'), may hold values from 0 to 3
- fit_count: int32 [4], P('sec'), may hold values from 6 to 12, as said below
- fit_blocks: float32 [4, 12, 128, 128], P('sec'), may hold values from -0.25 to 0.25
- border_map: int32 [4, 2], P('sec'), may hold values from 0 to 3
- coulomb_metric_root: float32 [4, 512, 512], P('sec'), may hold values from -0.25 to 0.25
- pair_list: int32 [4, 3, 2], P('sec'), may hold values from 0 to 3
- times: float32 [8], replicated, may hold values from 0.05 to 8
- time_weights: float32 [8], replicated, may hold values from 0.2 to 1
- freqs: float32 [8], replicated, may hold values from 0.05 to 8
Outputs:
- screened: float32 [8, 4, 3, 128, 128], P('tm', 'sec')
The draws below stay inside these ranges and needn't reach their ends.
Inputs may be any that keep to these rules, and one draw needn't show every extreme that they name: `fit_count`: some section lists exactly 12 fit blocks; entries at or past a section's count are unused. Within a section, the listed (fit_rows, fit_cols) positions are all different.
All inputs are finite; a program needn't handle non-finite values.
Results may differ from the reference program's by a relative error of at most 0.0003.
Values sent between devices are 32-bit elements; how exact they have to be, the bound alone decides.
No kernel may reach another device: no remote copies, remote signals or barrier semaphores. Data moves between devices by JAX's collectives and lax.ppermute only.
A program may use at most 128 MiB of HBM per device.

```python
import math
import jax
import jax.numpy as jnp
from jax import lax

BLOCK = 128
OWN_BLK = 4
BORDER_BLK = 2
PT_BLK = 4
MOST_FIT_BLOCKS = 12
PAIRS = 3
TIMES = 8
FREQS = 8
SECTIONS = 4
OWN_ROWS = 512
PT_ROWS = 512


def fit_positions(key):
    base = jax.random.fold_in(key, 7)
    section_keys = jax.random.split(base, SECTIONS)
    grid_size = (OWN_BLK + BORDER_BLK) * PT_BLK

    def one_section(section_key):
        return jax.random.permutation(section_key, grid_size)[:MOST_FIT_BLOCKS]
    return jax.vmap(one_section)(section_keys).astype(jnp.int32)


def draw_fit_rows(key, part):
    return (fit_positions(key) // PT_BLK).astype(jnp.int32)


def draw_fit_cols(key, part):
    return (fit_positions(key) % PT_BLK).astype(jnp.int32)


def draw_fit_count(key, part):
    key_counts, key_fullest = jax.random.split(key)
    counts = jax.random.randint(key_counts, (SECTIONS,), MOST_FIT_BLOCKS // 2, MOST_FIT_BLOCKS + 1)
    fullest = jax.random.randint(key_fullest, (), 0, SECTIONS)
    return jnp.where(jnp.arange(SECTIONS) == fullest, MOST_FIT_BLOCKS, counts).astype(jnp.int32)


def with_ends(array, own_key, low, high):
    longest = array.shape.index(max(array.shape))
    spots = []
    for shift in (0, 1):
        where = [jax.random.randint(jax.random.fold_in(own_key, axis), (), 0, length) for axis, length in enumerate(array.shape)]
        where[longest] = (where[longest] + shift) % array.shape[longest]
        spots.append(tuple(where))
    return array.at[spots[0]].set(low).at[spots[1]].set(high)


def block_levels(rng, shape, cuts, least, largest):
    factor_of, own = 1.0, jax.random.fold_in(rng, 6)
    for dim, parts in cuts:
        steps = jnp.exp(jax.random.uniform(jax.random.fold_in(own, dim), (parts,), jnp.float32, least / len(cuts), largest / len(cuts)))
        factor_of = factor_of * jnp.repeat(steps, shape[dim] // parts).reshape([-1 if axis == dim else 1 for axis in range(len(shape))])
    return factor_of


def centred(rng, extent, scale, reach, shards=(), dtype=jnp.bfloat16):
    array = scale * jax.random.normal(rng, extent, jnp.float32)
    if shards:
        array = array * block_levels(rng, extent, shards, -0.22, 0.18)
    return jnp.clip(array, -reach, reach).astype(dtype)


def setup_inputs(seed: int = 0) -> dict:
    arg_keys = jax.random.split(jax.random.key(seed), 13)
    return {
        "green_occ": centred(arg_keys[0], (TIMES, SECTIONS, PT_ROWS, PT_ROWS), 1.0, 6.0, ((0, 8), (1, 4)), jnp.float32),
        "virtual_green_time": centred(arg_keys[1], (TIMES, SECTIONS, PT_ROWS, PT_ROWS), 1.0, 6.0, ((0, 8), (1, 4)), jnp.float32),
        "fit_rows": draw_fit_rows(jax.random.fold_in(arg_keys[12], 71), 0),
        "fit_cols": draw_fit_cols(jax.random.fold_in(arg_keys[12], 71), 0),
        "fit_count": draw_fit_count(jax.random.fold_in(arg_keys[12], 71), 0),
        "fit_blocks": centred(arg_keys[5], (SECTIONS, MOST_FIT_BLOCKS, BLOCK, BLOCK), PT_ROWS ** -0.5, 0.25, ((0, 4),), jnp.float32),
        "border_map": with_ends(jax.random.randint(arg_keys[6], (SECTIONS, BORDER_BLK), 0, OWN_BLK), jax.random.fold_in(arg_keys[6], 1), 0, OWN_BLK - 1).astype(jnp.int32),
        "coulomb_metric_root": centred(arg_keys[7], (SECTIONS, OWN_ROWS, OWN_ROWS), OWN_ROWS ** -0.5, 0.25, ((0, 4),), jnp.float32),
        "pair_list": with_ends(jax.random.randint(arg_keys[8], (SECTIONS, PAIRS, 2), 0, OWN_BLK), jax.random.fold_in(arg_keys[8], 1), 0, OWN_BLK - 1).astype(jnp.int32),
        "times": jnp.clip(jnp.exp(jax.random.uniform(arg_keys[9], (TIMES,), jnp.float32, math.log(0.05), math.log(8.0))), 0.05, 8.0),
        "time_weights": jnp.clip(jax.random.uniform(arg_keys[10], (TIMES,), jnp.float32, 0.2, 1.0), 0.2, 1.0),
        "freqs": jnp.clip(jnp.exp(jax.random.uniform(arg_keys[11], (FREQS,), jnp.float32, math.log(0.05), math.log(8.0))), 0.05, 8.0),
    }


LARGEST_FIT = lax.Precision.HIGHEST


def fit_matrix(row_ids, col_ids, live_count, fit_values):
    ext_blocks = OWN_BLK + BORDER_BLK
    live = (jnp.arange(MOST_FIT_BLOCKS) < live_count).astype(jnp.float32)
    row_hot = (row_ids[:, None] == jnp.arange(ext_blocks)[None, :]).astype(jnp.float32) * live[:, None]
    col_hot = (col_ids[:, None] == jnp.arange(PT_BLK)[None, :]).astype(jnp.float32)
    dense = jnp.einsum('fe,fk,fab->eakb', row_hot, col_hot, fit_values, precision=LARGEST_FIT)
    return dense.reshape(ext_blocks * BLOCK, PT_BLK * BLOCK)


def section_terms(inputs):
    occupied, virtual, row_ids, col_ids, live_count, fit_values = inputs
    dense = fit_matrix(row_ids, col_ids, live_count, fit_values)

    def one_time(paired):
        product = paired[0] * paired[1]
        left_factor = jnp.dot(dense, product, precision=LARGEST_FIT)
        return jnp.dot(left_factor, dense.T, precision=LARGEST_FIT)

    extended = lax.map(one_time, (occupied, virtual))
    own_rows = OWN_BLK * BLOCK
    return extended[:, :own_rows, :own_rows], extended[:, own_rows:, own_rows:]


def reference(green_occ, virtual_green_time, fit_rows, fit_cols, fit_count, fit_blocks, border_map, coulomb_metric_root, pair_list, times, time_weights, freqs):
    own_part, border = lax.map(section_terms, (jnp.swapaxes(green_occ, 0, 1), jnp.swapaxes(virtual_green_time, 0, 1), fit_rows, fit_cols, fit_count, fit_blocks))
    sections = own_part.shape[0]
    slots = own_part.shape[1]
    incoming = jnp.roll(border, 1, axis=0)
    spread = (border_map[:, :, None] == jnp.arange(OWN_BLK)[None, None, :]).astype(jnp.float32)
    incoming = incoming.reshape(sections, slots, BORDER_BLK, BLOCK, BORDER_BLK, BLOCK)
    border_block_sum = jnp.einsum('sja,stjmkn,skb->stambn', spread, incoming, spread, precision=LARGEST_FIT)
    polarization = own_part + border_block_sum.reshape(own_part.shape)
    cosine = time_weights[None, :] * jnp.cos(freqs[:, None] * times[None, :])
    spectral_polar = jnp.einsum('wt,stmn->swmn', cosine, polarization, precision=LARGEST_FIT)
    left_factor = jnp.einsum('pbe,poec->pobc', coulomb_metric_root, spectral_polar, precision=LARGEST_FIT)
    projected_fit = jnp.einsum('ekah,eoh->ekao', left_factor, coulomb_metric_root, precision=LARGEST_FIT)
    projected_fit = projected_fit.reshape(sections, projected_fit.shape[1], OWN_BLK, BLOCK, OWN_BLK, BLOCK)
    pick_rows = (pair_list[:, :, 0][:, :, None] == jnp.arange(OWN_BLK)[None, None, :]).astype(jnp.float32)
    pick_cols = (pair_list[:, :, 1][:, :, None] == jnp.arange(OWN_BLK)[None, None, :]).astype(jnp.float32)
    return jnp.einsum('spa,swambn,spb->wspmn', pick_rows, projected_fit, pick_cols, precision=LARGEST_FIT)
```

```python
import functools

import jax
import jax.numpy as jnp
from jax import lax
from jax.experimental import pallas as pl
from jax.experimental.pallas import tpu as pltpu
from jax.sharding import PartitionSpec as P

OWN_BLK = 4
BORDER_BLK = 2
CORES = 2

VMEM = pl.BlockSpec(memory_space=pltpu.VMEM)
SMEM = pl.BlockSpec(memory_space=pltpu.SMEM)
NN = (((1,), (0,)), ((), ()))
NT = (((1,), (1,)), ((), ()))


def split(x):
    high = x.astype(jnp.bfloat16)
    return high, (x - high.astype(jnp.float32)).astype(jnp.bfloat16)


def dot3(a, b, dims):
    mm = functools.partial(
        lax.dot_general, dimension_numbers=dims, preferred_element_type=jnp.float32
    )
    return mm(a[0], b[0]) + (mm(a[0], b[1]) + mm(a[1], b[0]))


def place_fit(rows, cols, count, blocks, high_ref, low_ref, first, last):
    order = blocks.shape[-1]
    high_ref[...] = jnp.zeros(high_ref.shape, high_ref.dtype)
    low_ref[...] = jnp.zeros(low_ref.shape, low_ref.dtype)
    for f in range(blocks.shape[0]):
        row = rows[0, f]

        @pl.when((f < count[0]) & (row >= first) & (row < last))
        def _():
            high, low = split(blocks[f])
            at_row = pl.ds(pl.multiple_of((row - first) * order, order), order)
            at_col = pl.ds(pl.multiple_of(cols[0, f] * order, order), order)
            high_ref[at_row, at_col] = high
            low_ref[at_row, at_col] = low


def border_kernel(rows, cols, count, occ, virt, blocks, out, fit_high, fit_low):
    place_fit(rows, cols, count, blocks, fit_high, fit_low, OWN_BLK, OWN_BLK + BORDER_BLK)
    product = split(occ[...] * virt[...])
    fit = (fit_high[...], fit_low[...])
    left = split(dot3(fit, product, NN))
    out[...] = dot3(left, fit, NT)


def own_kernel(
    rows, cols, count, border_map, pairs, occ, virt, blocks, metric,
    out, edge_high, edge_low,
    fit_high, fit_low, proj_high, proj_low, pick_high, pick_low,
):
    order = blocks.shape[-1]
    place_fit(rows, cols, count, blocks, fit_high, fit_low, 0, OWN_BLK)
    metric_parts = split(metric[...])
    for j in range(BORDER_BLK):
        at = pl.ds(pl.multiple_of(border_map[0, j] * order, order), order)
        high, low = split(metric[:, at])
        edge_high[:, j * order : (j + 1) * order] = high
        edge_low[:, j * order : (j + 1) * order] = low
    high, low = split(dot3(metric_parts, (fit_high[...], fit_low[...]), NN))
    proj_high[...] = high
    proj_low[...] = low
    count_pairs = out.shape[0]
    for p in range(count_pairs):
        at = pl.ds(pl.multiple_of(pairs[0, p, 0] * order, order), order)
        pick_high[p * order : (p + 1) * order, :] = proj_high[at, :]
        pick_low[p * order : (p + 1) * order, :] = proj_low[at, :]
    product = split(occ[...] * virt[...])
    left = dot3((pick_high[...], pick_low[...]), product, NN)
    for p in range(count_pairs):
        at = pl.ds(pl.multiple_of(pairs[0, p, 1] * order, order), order)
        out[p] = dot3(
            split(left[p * order : (p + 1) * order, :]), (proj_high[at, :], proj_low[at, :]), NT
        )


def join_kernel(pairs, place, border, own, edge_high, edge_low, *refs):
    pick_high, pick_low, total = refs[-3:]
    outs = refs[:-3]
    count_pairs, order, _ = own.shape
    for p in range(count_pairs):
        at = pl.ds(pl.multiple_of(pairs[0, p, 0] * order, order), order)
        pick_high[p * order : (p + 1) * order, :] = edge_high[at, :]
        pick_low[p * order : (p + 1) * order, :] = edge_low[at, :]
    left = dot3((pick_high[...], pick_low[...]), split(border[...]), NN)
    for p in range(count_pairs):
        at = pl.ds(pl.multiple_of(pairs[0, p, 1] * order, order), order)
        total[p] = own[p] + dot3(
            split(left[p * order : (p + 1) * order, :]), (edge_high[at, :], edge_low[at, :]), NT
        )
    share = outs[0].shape[1]
    for k, out in enumerate(outs):
        at = pl.ds(pl.multiple_of((place[0] ^ k) * share, share), share)
        out[...] = total[:, at, :]


def combine_kernel(place, cosine, *refs):
    chips = len(refs) // 3
    mine, other, outs = refs[:chips], refs[chips : 2 * chips], refs[2 * chips :]
    chip, core = place[0], place[1]
    times = CORES * chips
    shape = outs[0].shape
    for k in range(chips):
        freq = ((chip ^ k) * CORES + core) * times
        total = jnp.zeros(shape, jnp.float32)
        for j in range(chips):
            at = freq + (chip ^ j) * CORES
            total += cosine[at + core] * mine[j][...] + cosine[at + 1 - core] * other[j][...]
        outs[k][...] = total


def gather_kernel(place, *refs):
    out = refs[-1]
    for k, part in enumerate(refs[:-1]):
        share = part.shape[1]
        at = pl.ds(pl.multiple_of((place[0] ^ k) * share, share), share)
        out[0, 0, :, at, :] = part[...]


def on_device(
    green_occ,
    virtual_green_time,
    fit_rows,
    fit_cols,
    fit_count,
    fit_blocks,
    border_map,
    coulomb_metric_root,
    pair_list,
    times,
    time_weights,
    freqs,
):
    points = green_occ.shape[-1]
    order = fit_blocks.shape[-1]
    own_rows = OWN_BLK * order
    edge_rows = BORDER_BLK * order
    pairs = pair_list.shape[1]
    devices = lax.axis_size("tm")
    chips = devices // CORES
    share = order // chips
    f32, bf16 = jnp.float32, jnp.bfloat16
    occ, virt = green_occ[0, 0], virtual_green_time[0, 0]
    blocks, metric = fit_blocks[0], coulomb_metric_root[0]
    index = lax.axis_index("tm")
    place = jnp.stack([index // CORES, index % CORES]).astype(jnp.int32)
    cosine = (time_weights[None, :] * jnp.cos(freqs[:, None] * times[None, :])).reshape(-1)

    border = pl.pallas_call(
        border_kernel,
        out_shape=jax.ShapeDtypeStruct((edge_rows, edge_rows), f32),
        in_specs=[SMEM] * 3 + [VMEM] * 3,
        out_specs=VMEM,
        scratch_shapes=[pltpu.VMEM((edge_rows, points), bf16)] * 2,
        cost_estimate=pl.CostEstimate(flops=10**9, bytes_accessed=3 << 20, transcendentals=0),
        name="border",
    )(fit_rows, fit_cols, fit_count, occ, virt, blocks)
    sections = lax.axis_size("sec")
    border = lax.ppermute(border, "sec", [(i, (i + 1) % sections) for i in range(sections)])

    own, edge_high, edge_low = pl.pallas_call(
        own_kernel,
        out_shape=(
            jax.ShapeDtypeStruct((pairs, order, order), f32),
            jax.ShapeDtypeStruct((own_rows, edge_rows), bf16),
            jax.ShapeDtypeStruct((own_rows, edge_rows), bf16),
        ),
        in_specs=[SMEM] * 5 + [VMEM] * 4,
        out_specs=(VMEM,) * 3,
        scratch_shapes=[pltpu.VMEM((own_rows, points), bf16)] * 4
        + [pltpu.VMEM((pairs * order, points), bf16)] * 2,
        cost_estimate=pl.CostEstimate(flops=2 * 10**9, bytes_accessed=5 << 20, transcendentals=0),
        name="own",
    )(fit_rows, fit_cols, fit_count, border_map, pair_list, occ, virt, blocks, metric)

    part = jax.ShapeDtypeStruct((pairs, share, order), f32)
    parts = pl.pallas_call(
        join_kernel,
        out_shape=(part,) * chips,
        in_specs=[SMEM] * 2 + [VMEM] * 4,
        out_specs=(VMEM,) * chips,
        scratch_shapes=[pltpu.VMEM((pairs * order, edge_rows), bf16)] * 2
        + [pltpu.VMEM((pairs, order, order), f32)],
        name="join",
    )(pair_list, place, border, own, edge_high, edge_low)

    def across(x, k):
        return lax.ppermute(x, "tm", [(i, i ^ (CORES * k)) for i in range(devices)])

    def swap(x):
        return lax.ppermute(x, "tm", [(i, i ^ 1) for i in range(devices)])

    mine = [parts[0]] + [across(parts[k], k) for k in range(1, chips)]
    other = [swap(x) for x in mine]
    parts = pl.pallas_call(
        combine_kernel,
        out_shape=(part,) * chips,
        in_specs=[SMEM] * 2 + [VMEM] * (2 * chips),
        out_specs=(VMEM,) * chips,
        name="combine",
    )(place, cosine, *mine, *other)
    parts = [parts[0]] + [across(parts[k], k) for k in range(1, chips)]
    return pl.pallas_call(
        gather_kernel,
        out_shape=jax.ShapeDtypeStruct((1, 1, pairs, order, order), f32),
        in_specs=[SMEM] + [VMEM] * chips,
        out_specs=VMEM,
        name="gather",
    )(place, *parts)


def solution(mesh):
    return jax.shard_map(
        on_device,
        mesh=mesh,
        in_specs=(
            P("tm", "sec", None, None),
            P("tm", "sec", None, None),
            P("sec", None),
            P("sec", None),
            P("sec"),
            P("sec", None, None, None),
            P("sec", None),
            P("sec", None, None),
            P("sec", None, None),
            P(),
            P(),
            P(),
        ),
        out_specs=P("tm", "sec", None, None, None),
        check_vma=False,
    )
```

```python
import functools

import jax
import jax.numpy as jnp
from jax import lax
from jax.experimental import pallas as pl
from jax.experimental.pallas import tpu as pltpu
from jax.sharding import PartitionSpec as P


OWN_BLK = 4
BORDER_BLK = 2
CORES = 2
SUBLANES = 8

VMEM = pl.BlockSpec(memory_space=pltpu.VMEM)
SMEM = pl.BlockSpec(memory_space=pltpu.SMEM)
ANY = pl.BlockSpec(memory_space=pl.ANY)
HBM = pl.BlockSpec(memory_space=pltpu.HBM)
CHUNKS = 2
VMEM_LIMIT = 16 << 20


NN = (((1,), (0,)), ((), ()))
NT = (((1,), (1,)), ((), ()))


def split(x):
    high = x.astype(jnp.bfloat16)
    return high, (x - high.astype(jnp.float32)).astype(jnp.bfloat16)


def dot3(a, b, dims):
    mm = functools.partial(
        lax.dot_general, dimension_numbers=dims, preferred_element_type=jnp.float32
    )
    return mm(a[0], b[0]) + (mm(a[0], b[1]) + mm(a[1], b[0]))


def place_fit(rows, cols, count, blocks, high_ref, low_ref, first, last):
    order = blocks.shape[-1]
    high_ref[...] = jnp.zeros(high_ref.shape, high_ref.dtype)
    low_ref[...] = jnp.zeros(low_ref.shape, low_ref.dtype)
    for f in range(blocks.shape[0]):
        row = rows[0, f]

        @pl.when((f < count[0]) & (row >= first) & (row < last))
        def _():
            high, low = split(blocks[f])
            at_row = pl.ds(pl.multiple_of((row - first) * order, order), order)
            at_col = pl.ds(pl.multiple_of(cols[0, f] * order, order), order)
            high_ref[at_row, at_col] = high
            low_ref[at_row, at_col] = low


def border_kernel(
    count, rows_in, cols_in, occ, virt, blocks, out, high_out, low_out,
    rows, cols, occ_buf, virt_buf, blocks_buf, fit_high, fit_low, sems,
):
    points = occ.shape[-1]
    step = points // CHUNKS
    first = [
        pltpu.make_async_copy(src, dst, sems.at[2 * CHUNKS + i])
        for i, (src, dst) in enumerate(
            ((rows_in, rows), (cols_in, cols), (blocks.at[0], blocks_buf))
        )
    ]
    for fetch in first:
        fetch.start()
    fetches = []
    for c in range(CHUNKS):
        at = slice(c * step, (c + 1) * step)
        fetches.append(
            [
                pltpu.make_async_copy(src.at[0, 0, at], dst.at[at], sems.at[2 * c + i])
                for i, (src, dst) in enumerate(((occ, occ_buf), (virt, virt_buf)))
            ]
        )
        for fetch in fetches[c]:
            fetch.start()
    for fetch in first:
        fetch.wait()
    place_fit(rows, cols, count, blocks_buf, fit_high, fit_low, OWN_BLK, OWN_BLK + BORDER_BLK)
    left = None
    for c in range(CHUNKS):
        at = slice(c * step, (c + 1) * step)
        for fetch in fetches[c]:
            fetch.wait()
        product = split(occ_buf[at] * virt_buf[at])
        high_out[at], low_out[at] = product
        term = dot3((fit_high[:, at], fit_low[:, at]), product, NN)
        left = term if left is None else left + term
    out[...] = dot3(split(left), (fit_high[...], fit_low[...]), NT)


def own_kernel(
    rows, cols, count, border_map, pairs, cosine, product_high, product_low, blocks, metric,
    out, row_high, row_low, col_high, col_low, weight,
    fit_high, fit_low, proj_high, proj_low, pick_high, pick_low, edge,
):
    order = blocks.shape[-1]
    place_fit(rows, cols, count, blocks, fit_high, fit_low, 0, OWN_BLK)
    for j in range(BORDER_BLK):
        at = pl.ds(pl.multiple_of(border_map[0, j] * order, order), order)
        edge[:, j * order : (j + 1) * order] = metric[:, at]
    high, low = split(dot3(split(metric[...]), (fit_high[...], fit_low[...]), NN))
    proj_high[...] = high
    proj_low[...] = low
    count_pairs = out.shape[0]
    for p in range(count_pairs):
        here = slice(p * order, (p + 1) * order)
        at = pl.ds(pl.multiple_of(pairs[0, 0, p] * order, order), order)
        pick_high[here, :] = proj_high[at, :]
        pick_low[here, :] = proj_low[at, :]
        row_high[here, :], row_low[here, :] = split(edge[at, :])
        at = pl.ds(pl.multiple_of(pairs[0, 1, p] * order, order), order)
        col_high[here, :], col_low[here, :] = split(edge[at, :])
    left = dot3(
        (pick_high[...], pick_low[...]), (product_high[...], product_low[...]), NN
    )
    for p in range(count_pairs):
        at = pl.ds(pl.multiple_of(pairs[0, 1, p] * order, order), order)
        out[p] = dot3(
            split(left[p * order : (p + 1) * order, :]), (proj_high[at, :], proj_low[at, :]), NT
        )
    index = lax.axis_index("tm")
    chip, core = index // CORES, index % CORES
    chips = weight.shape[0]
    for k in range(chips):
        freq = (chip ^ k) * CORES + core
        for j in range(chips):
            at = (chip ^ j) * CORES
            weight[k, j, 0] = jnp.full(weight.shape[3:], cosine[freq, at + core])
            weight[k, j, 1] = jnp.full(weight.shape[3:], cosine[freq, at + 1 - core])


def join_kernel(border, own, row_high, row_low, col_high, col_low, *refs):
    total, outs = refs[-1], refs[:-1]
    chip = lax.axis_index("tm") // CORES
    count_pairs, order, _ = own.shape
    left = dot3((row_high[...], row_low[...]), split(border[...]), NN)
    for p in range(count_pairs):
        here = slice(p * order, (p + 1) * order)
        total[p] = own[p] + dot3(split(left[here]), (col_high[here], col_low[here]), NT)
    share = outs[0].shape[1]
    for k, out in enumerate(outs):
        at = pl.ds(pl.multiple_of((chip ^ k) * share, share), share)
        out[...] = total[:, at, :]


def combine_kernel(weight, *refs):
    chips = len(refs) // 3
    mine, other, outs = refs[:chips], refs[chips : 2 * chips], refs[2 * chips :]
    for k in range(chips):
        total = jnp.zeros(outs[k].shape, jnp.float32)
        for j in range(chips):
            total += weight[k, j, 0] * mine[j][...]
            total += weight[k, j, 1] * other[j][...]
        outs[k][...] = total


def gather_kernel(*refs):
    parts, out, sems = refs[:-2], refs[-2], refs[-1]
    chip = lax.axis_index("tm") // CORES
    copies = []
    for k, part in enumerate(parts):
        share = part.shape[1]
        at = pl.ds(pl.multiple_of((chip ^ k) * share, share), share)
        copies.append(pltpu.make_async_copy(part, out.at[0, 0, :, at, :], sems.at[k]))
        copies[k].start()
    for copy in copies:
        copy.wait()


def in_vmem(x):
    return pltpu.with_memory_space_constraint(x, pltpu.VMEM)


def in_hbm(x):
    return pltpu.with_memory_space_constraint(x, pltpu.HBM)


def on_device(
    green_occ,
    virtual_green_time,
    fit_rows,
    fit_cols,
    fit_count,
    fit_blocks,
    border_map,
    coulomb_metric_root,
    pair_list,
    times,
    time_weights,
    freqs,
):
    points = green_occ.shape[-1]
    order = fit_blocks.shape[-1]
    own_rows = OWN_BLK * order
    edge_rows = BORDER_BLK * order
    pairs = pair_list.shape[1]
    devices = lax.axis_size("tm")
    chips = devices // CORES
    share = order // chips
    f32, bf16 = jnp.float32, jnp.bfloat16
    cosine = time_weights[None, :] * jnp.cos(freqs[:, None] * times[None, :])
    pair_rows_cols = jnp.swapaxes(pair_list, 1, 2)
    limit = pltpu.CompilerParams(vmem_limit_bytes=VMEM_LIMIT)

    border, product_high, product_low = pl.pallas_call(
        border_kernel,
        out_shape=(
            pltpu.VMEM((edge_rows, edge_rows), f32),
            pltpu.VMEM((points, points), bf16),
            pltpu.VMEM((points, points), bf16),
        ),
        in_specs=[SMEM] + [HBM] * 5,
        out_specs=(VMEM,) * 3,
        scratch_shapes=[pltpu.SMEM(fit_rows.shape, jnp.int32)] * 2
        + [pltpu.VMEM((points, points), f32)] * 2
        + [pltpu.VMEM(fit_blocks.shape[1:], f32)]
        + [pltpu.VMEM((edge_rows, points), bf16)] * 2
        + [pltpu.SemaphoreType.DMA((2 * CHUNKS + 3,))],
        cost_estimate=pl.CostEstimate(flops=10**9, bytes_accessed=3 << 20, transcendentals=0),
        compiler_params=limit,
        name="border",
    )(
        fit_count, in_hbm(fit_rows), in_hbm(fit_cols),
        in_hbm(green_occ), in_hbm(virtual_green_time), in_hbm(fit_blocks),
    )
    sections = lax.axis_size("sec")
    border = lax.ppermute(border, "sec", [(i, (i + 1) % sections) for i in range(sections)])

    edge = pltpu.VMEM((pairs * order, edge_rows), bf16)
    own, row_high, row_low, col_high, col_low, weight = pl.pallas_call(
        own_kernel,
        out_shape=(pltpu.VMEM((pairs, order, order), f32),)
        + (edge,) * 4
        + (pltpu.VMEM((chips, chips, CORES, SUBLANES, order), f32),),
        in_specs=[SMEM] * 6 + [VMEM] * 4,
        out_specs=(VMEM,) * 6,
        scratch_shapes=[pltpu.VMEM((own_rows, points), bf16)] * 4
        + [pltpu.VMEM((pairs * order, points), bf16)] * 2
        + [pltpu.VMEM((own_rows, edge_rows), f32)],
        cost_estimate=pl.CostEstimate(flops=2 * 10**9, bytes_accessed=5 << 20, transcendentals=0),
        compiler_params=limit,
        name="own",
    )(
        fit_rows, fit_cols, fit_count, border_map, pair_rows_cols, cosine,
        in_vmem(product_high), in_vmem(product_low),
        in_vmem(fit_blocks[0]), in_vmem(coulomb_metric_root[0]),
    )

    part = pltpu.VMEM((pairs, share, order), f32)
    parts = pl.pallas_call(
        join_kernel,
        out_shape=(part,) * chips,
        in_specs=[VMEM] * 6,
        out_specs=(VMEM,) * chips,
        scratch_shapes=[pltpu.VMEM((pairs, order, order), f32)],
        compiler_params=limit,
        name="join",
    )(*map(in_vmem, (border, own, row_high, row_low, col_high, col_low)))

    def across(x, k):
        return lax.ppermute(x, "tm", [(i, i ^ (CORES * k)) for i in range(devices)])

    def swap(x):
        return lax.ppermute(x, "tm", [(i, i ^ 1) for i in range(devices)])

    mine = [parts[0]] + [across(parts[k], k) for k in range(1, chips)]
    other = [swap(x) for x in mine]
    tiles = pltpu.VMEM((pairs * share // SUBLANES, SUBLANES, order), f32)
    parts = pl.pallas_call(
        combine_kernel,
        out_shape=(tiles,) * chips,
        in_specs=[VMEM] * (2 * chips + 1),
        out_specs=(VMEM,) * chips,
        compiler_params=limit,
        name="combine",
    )(*(in_vmem(x.reshape(tiles.shape) if x.ndim == 3 else x) for x in (weight, *mine, *other)))
    parts = [x.reshape(part.shape) for x in parts]
    parts = [parts[0]] + [across(parts[k], k) for k in range(1, chips)]
    return pl.pallas_call(
        gather_kernel,
        out_shape=jax.ShapeDtypeStruct((1, 1, pairs, order, order), f32),
        in_specs=[VMEM] * chips,
        out_specs=ANY,
        scratch_shapes=[pltpu.SemaphoreType.DMA((chips,))],
        compiler_params=limit,
        name="gather",
    )(*map(in_vmem, parts))


def solution(mesh):
    return jax.shard_map(
        on_device,
        mesh=mesh,
        in_specs=(
            P("tm", "sec", None, None),
            P("tm", "sec", None, None),
            P("sec", None),
            P("sec", None),
            P("sec"),
            P("sec", None, None, None),
            P("sec", None),
            P("sec", None, None),
            P("sec", None, None),
            P(),
            P(),
            P(),
        ),
        out_specs=P("tm", "sec", None, None, None),
        check_vma=False,
    )
```

```python
import functools

import jax
import jax.numpy as jnp
from jax import lax
from jax.experimental import pallas as pl
from jax.experimental.pallas import tpu as pltpu
from jax.sharding import PartitionSpec as P


OWN_BLK = 4
BORDER_BLK = 2
CORES = 2
SUBLANES = 8

VMEM = pl.BlockSpec(memory_space=pltpu.VMEM)
SMEM = pl.BlockSpec(memory_space=pltpu.SMEM)
ANY = pl.BlockSpec(memory_space=pl.ANY)
HBM = pl.BlockSpec(memory_space=pltpu.HBM)
CHUNKS = 2
VMEM_LIMIT = 16 << 20


ROUTES = ("xor", "ring")


NN = (((1,), (0,)), ((), ()))
NT = (((1,), (1,)), ((), ()))


def pick(flag, yes, no):
    return (yes if flag else no) if isinstance(flag, bool) else jnp.where(flag, yes, no)


def ring_place(chip, chips):
    return pick(chip % 2 == 1, (chip + 1) // 2, (chips - chip // 2) % chips)


def ring_chip(place, chips):
    return pick(place == 0, 0, pick(place <= chips // 2, 2 * place - 1, 2 * (chips - place)))


def to_chip(phase, chip, step, chips):
    if ROUTES[phase] == "xor":
        return chip ^ step
    return ring_chip((ring_place(chip, chips) + step) % chips, chips)


def from_chip(phase, chip, step, chips):
    if ROUTES[phase] == "xor":
        return chip ^ step
    return ring_chip((ring_place(chip, chips) + chips - step) % chips, chips)


def split(x):
    high = x.astype(jnp.bfloat16)
    return high, (x - high.astype(jnp.float32)).astype(jnp.bfloat16)


def dot3(a, b, dims):
    mm = functools.partial(
        lax.dot_general, dimension_numbers=dims, preferred_element_type=jnp.float32
    )
    return mm(a[0], b[0]) + (mm(a[0], b[1]) + mm(a[1], b[0]))


def place_fit(rows, cols, count, blocks, high_ref, low_ref, first, last):
    order = blocks.shape[-1]
    high_ref[...] = jnp.zeros(high_ref.shape, high_ref.dtype)
    low_ref[...] = jnp.zeros(low_ref.shape, low_ref.dtype)
    for f in range(blocks.shape[0]):
        row = rows[0, f]

        @pl.when((f < count[0]) & (row >= first) & (row < last))
        def _():
            high, low = split(blocks[f])
            at_row = pl.ds(pl.multiple_of((row - first) * order, order), order)
            at_col = pl.ds(pl.multiple_of(cols[0, f] * order, order), order)
            high_ref[at_row, at_col] = high
            low_ref[at_row, at_col] = low


def border_kernel(
    count, rows_in, cols_in, occ, virt, blocks, out, high_out, low_out, blocks_buf,
    rows, cols, occ_buf, virt_buf, fit_high, fit_low, sems,
):
    points = occ.shape[-1]
    step = points // CHUNKS
    first = [
        pltpu.make_async_copy(src, dst, sems.at[2 * CHUNKS + i])
        for i, (src, dst) in enumerate(
            ((rows_in, rows), (cols_in, cols), (blocks.at[0], blocks_buf))
        )
    ]
    for fetch in first:
        fetch.start()
    fetches = []
    for c in range(CHUNKS):
        at = slice(c * step, (c + 1) * step)
        fetches.append(
            [
                pltpu.make_async_copy(src.at[0, 0, at], dst.at[at], sems.at[2 * c + i])
                for i, (src, dst) in enumerate(((occ, occ_buf), (virt, virt_buf)))
            ]
        )
        for fetch in fetches[c]:
            fetch.start()
    for fetch in first:
        fetch.wait()
    place_fit(rows, cols, count, blocks_buf, fit_high, fit_low, OWN_BLK, OWN_BLK + BORDER_BLK)
    left = None
    for c in range(CHUNKS):
        at = slice(c * step, (c + 1) * step)
        for fetch in fetches[c]:
            fetch.wait()
        product = split(occ_buf[at] * virt_buf[at])
        high_out[at], low_out[at] = product
        term = dot3((fit_high[:, at], fit_low[:, at]), product, NN)
        left = term if left is None else left + term
    out[...] = dot3(split(left), (fit_high[...], fit_low[...]), NT)


def own_kernel(
    rows, cols, count, border_map, pairs, cosine, product_high, product_low, blocks, metric,
    out, row_high, row_low, col_high, col_low, weight,
    fit_high, fit_low, proj_high, proj_low, pick_high, pick_low, edge,
):
    order = blocks.shape[-1]
    place_fit(rows, cols, count, blocks, fit_high, fit_low, 0, OWN_BLK)
    for j in range(BORDER_BLK):
        at = pl.ds(pl.multiple_of(border_map[0, j] * order, order), order)
        edge[:, j * order : (j + 1) * order] = metric[:, at]
    high, low = split(dot3(split(metric[...]), (fit_high[...], fit_low[...]), NN))
    proj_high[...] = high
    proj_low[...] = low
    count_pairs = out.shape[0]
    for p in range(count_pairs):
        here = slice(p * order, (p + 1) * order)
        at = pl.ds(pl.multiple_of(pairs[0, 0, p] * order, order), order)
        pick_high[here, :] = proj_high[at, :]
        pick_low[here, :] = proj_low[at, :]
        row_high[here, :], row_low[here, :] = split(edge[at, :])
        at = pl.ds(pl.multiple_of(pairs[0, 1, p] * order, order), order)
        col_high[here, :], col_low[here, :] = split(edge[at, :])
    left = dot3(
        (pick_high[...], pick_low[...]), (product_high[...], product_low[...]), NN
    )
    for p in range(count_pairs):
        at = pl.ds(pl.multiple_of(pairs[0, 1, p] * order, order), order)
        out[p] = dot3(
            split(left[p * order : (p + 1) * order, :]), (proj_high[at, :], proj_low[at, :]), NT
        )
    index = lax.axis_index("tm")
    chip, core = index // CORES, index % CORES
    chips = weight.shape[0]
    for k in range(chips):
        freq = to_chip(1, chip, k, chips) * CORES + core
        for j in range(chips):
            at = from_chip(0, chip, j, chips) * CORES
            weight[k, j, 0] = jnp.full(weight.shape[3:], cosine[freq, at + core])
            weight[k, j, 1] = jnp.full(weight.shape[3:], cosine[freq, at + 1 - core])


def join_kernel(border, own, row_high, row_low, col_high, col_low, *refs):
    total, outs = refs[-1], refs[:-1]
    chip = lax.axis_index("tm") // CORES
    count_pairs, order, _ = own.shape
    left = dot3((row_high[...], row_low[...]), split(border[...]), NN)
    for p in range(count_pairs):
        here = slice(p * order, (p + 1) * order)
        total[p] = own[p] + dot3(split(left[here]), (col_high[here], col_low[here]), NT)
    share = outs[0].shape[1]
    for k, out in enumerate(outs):
        at = pl.ds(pl.multiple_of(to_chip(0, chip, k, len(outs)) * share, share), share)
        out[...] = total[:, at, :]


def combine_kernel(weight, *refs):
    chips = len(refs) // 3
    mine, other, outs = refs[:chips], refs[chips : 2 * chips], refs[2 * chips :]
    for k in range(chips):
        total = jnp.zeros(outs[k].shape, jnp.float32)
        for j in range(chips):
            total += weight[k, j, 0] * mine[j][...]
            total += weight[k, j, 1] * other[j][...]
        outs[k][...] = total


def gather_kernel(*refs):
    parts, out, sems = refs[:-2], refs[-2], refs[-1]
    chip = lax.axis_index("tm") // CORES
    copies = []
    for k, part in enumerate(parts):
        share = part.shape[1]
        at = pl.ds(pl.multiple_of(from_chip(1, chip, k, len(parts)) * share, share), share)
        copies.append(pltpu.make_async_copy(part, out.at[0, 0, :, at, :], sems.at[k]))
        copies[k].start()
    for copy in copies:
        copy.wait()


def in_vmem(x):
    return pltpu.with_memory_space_constraint(x, pltpu.VMEM)


def in_hbm(x):
    return pltpu.with_memory_space_constraint(x, pltpu.HBM)


def on_device(
    green_occ,
    virtual_green_time,
    fit_rows,
    fit_cols,
    fit_count,
    fit_blocks,
    border_map,
    coulomb_metric_root,
    pair_list,
    times,
    time_weights,
    freqs,
):
    points = green_occ.shape[-1]
    order = fit_blocks.shape[-1]
    own_rows = OWN_BLK * order
    edge_rows = BORDER_BLK * order
    pairs = pair_list.shape[1]
    devices = lax.axis_size("tm")
    chips = devices // CORES
    share = order // chips
    f32, bf16 = jnp.float32, jnp.bfloat16
    cosine = time_weights[None, :] * jnp.cos(freqs[:, None] * times[None, :])
    pair_rows_cols = jnp.swapaxes(pair_list, 1, 2)
    limit = pltpu.CompilerParams(vmem_limit_bytes=VMEM_LIMIT)

    border, product_high, product_low, blocks = pl.pallas_call(
        border_kernel,
        out_shape=(
            pltpu.VMEM((edge_rows, edge_rows), f32),
            pltpu.VMEM((points, points), bf16),
            pltpu.VMEM((points, points), bf16),
            pltpu.VMEM(fit_blocks.shape[1:], f32),
        ),
        in_specs=[SMEM] + [HBM] * 5,
        out_specs=(VMEM,) * 4,
        scratch_shapes=[pltpu.SMEM(fit_rows.shape, jnp.int32)] * 2
        + [pltpu.VMEM((points, points), f32)] * 2
        + [pltpu.VMEM((edge_rows, points), bf16)] * 2
        + [pltpu.SemaphoreType.DMA((2 * CHUNKS + 3,))],
        cost_estimate=pl.CostEstimate(flops=10**9, bytes_accessed=3 << 20, transcendentals=0),
        compiler_params=limit,
        name="border",
    )(
        fit_count, in_hbm(fit_rows), in_hbm(fit_cols),
        in_hbm(green_occ), in_hbm(virtual_green_time), in_hbm(fit_blocks),
    )
    sections = lax.axis_size("sec")
    border = lax.ppermute(border, "sec", [(i, (i + 1) % sections) for i in range(sections)])

    edge = pltpu.VMEM((pairs * order, edge_rows), bf16)
    own, row_high, row_low, col_high, col_low, weight = pl.pallas_call(
        own_kernel,
        out_shape=(pltpu.VMEM((pairs, order, order), f32),)
        + (edge,) * 4
        + (pltpu.VMEM((chips, chips, CORES, SUBLANES, order), f32),),
        in_specs=[SMEM] * 6 + [VMEM] * 4,
        out_specs=(VMEM,) * 6,
        scratch_shapes=[pltpu.VMEM((own_rows, points), bf16)] * 4
        + [pltpu.VMEM((pairs * order, points), bf16)] * 2
        + [pltpu.VMEM((own_rows, edge_rows), f32)],
        cost_estimate=pl.CostEstimate(flops=2 * 10**9, bytes_accessed=5 << 20, transcendentals=0),
        compiler_params=limit,
        name="own",
    )(
        fit_rows, fit_cols, fit_count, border_map, pair_rows_cols, cosine,
        in_vmem(product_high), in_vmem(product_low),
        in_vmem(blocks), in_hbm(coulomb_metric_root[0]),
    )

    part = pltpu.VMEM((pairs, share, order), f32)
    parts = pl.pallas_call(
        join_kernel,
        out_shape=(part,) * chips,
        in_specs=[VMEM] * 6,
        out_specs=(VMEM,) * chips,
        scratch_shapes=[pltpu.VMEM((pairs, order, order), f32)],
        compiler_params=limit,
        name="join",
    )(*map(in_vmem, (border, own, row_high, row_low, col_high, col_low)))

    def across(x, k, phase):
        pairs_of = [
            (i, to_chip(phase, i // CORES, k, chips) * CORES + i % CORES) for i in range(devices)
        ]
        return lax.ppermute(x, "tm", pairs_of)

    def swap(x):
        return lax.ppermute(x, "tm", [(i, i ^ 1) for i in range(devices)])

    mine = [parts[0]] + [across(parts[k], k, 0) for k in range(1, chips)]
    other = [swap(x) for x in mine]
    tiles = pltpu.VMEM((pairs * share // SUBLANES, SUBLANES, order), f32)
    parts = pl.pallas_call(
        combine_kernel,
        out_shape=(tiles,) * chips,
        in_specs=[VMEM] * (2 * chips + 1),
        out_specs=(VMEM,) * chips,
        compiler_params=limit,
        name="combine",
    )(*(in_vmem(x.reshape(tiles.shape) if x.ndim == 3 else x) for x in (weight, *mine, *other)))
    parts = [x.reshape(part.shape) for x in parts]
    parts = [parts[0]] + [across(parts[k], k, 1) for k in range(1, chips)]
    return pl.pallas_call(
        gather_kernel,
        out_shape=jax.ShapeDtypeStruct((1, 1, pairs, order, order), f32),
        in_specs=[VMEM] * chips,
        out_specs=ANY,
        scratch_shapes=[pltpu.SemaphoreType.DMA((chips,))],
        compiler_params=limit,
        name="gather",
    )(*map(in_vmem, parts))


def solution(mesh):
    return jax.shard_map(
        on_device,
        mesh=mesh,
        in_specs=(
            P("tm", "sec", None, None),
            P("tm", "sec", None, None),
            P("sec", None),
            P("sec", None),
            P("sec"),
            P("sec", None, None, None),
            P("sec", None),
            P("sec", None, None),
            P("sec", None, None),
            P(),
            P(),
            P(),
        ),
        out_specs=P("tm", "sec", None, None, None),
        check_vma=False,
    )
```

```python
import functools

import jax
import jax.numpy as jnp
from jax import lax
from jax.experimental import pallas as pl
from jax.experimental.pallas import tpu as pltpu
from jax.sharding import PartitionSpec as P


OWN_BLK = 4
BORDER_BLK = 2
CORES = 2
SUBLANES = 8

VMEM = pl.BlockSpec(memory_space=pltpu.VMEM)
SMEM = pl.BlockSpec(memory_space=pltpu.SMEM)
ANY = pl.BlockSpec(memory_space=pl.ANY)
HBM = pl.BlockSpec(memory_space=pltpu.HBM)
CHUNKS = 2
VMEM_LIMIT = 16 << 20


ROUTES = ("xor", "ring")


NN = (((1,), (0,)), ((), ()))
NT = (((1,), (1,)), ((), ()))


def pick(flag, yes, no):
    return (yes if flag else no) if isinstance(flag, bool) else jnp.where(flag, yes, no)


def ring_place(chip, chips):
    return pick(chip % 2 == 1, (chip + 1) // 2, (chips - chip // 2) % chips)


def ring_chip(place, chips):
    return pick(place == 0, 0, pick(place <= chips // 2, 2 * place - 1, 2 * (chips - place)))


def to_chip(phase, chip, step, chips):
    if ROUTES[phase] == "xor":
        return chip ^ step
    return ring_chip((ring_place(chip, chips) + step) % chips, chips)


def from_chip(phase, chip, step, chips):
    if ROUTES[phase] == "xor":
        return chip ^ step
    return ring_chip((ring_place(chip, chips) + chips - step) % chips, chips)


def split(x):
    high = x.astype(jnp.bfloat16)
    return high, (x - high.astype(jnp.float32)).astype(jnp.bfloat16)


def dot3(a, b, dims):
    mm = functools.partial(
        lax.dot_general, dimension_numbers=dims, preferred_element_type=jnp.float32
    )
    return mm(a[0], b[0]) + (mm(a[0], b[1]) + mm(a[1], b[0]))


def dot3_halves(a, b, dims):
    half = a[0].shape[0] // 2
    return jnp.concatenate(
        [dot3((a[0][at], a[1][at]), b, dims) for at in (slice(0, half), slice(half, 2 * half))],
        axis=0,
    )


def place_fit(rows, cols, count, blocks, high_ref, low_ref, first, last):
    order = blocks.shape[-1]
    high_ref[...] = jnp.zeros(high_ref.shape, high_ref.dtype)
    low_ref[...] = jnp.zeros(low_ref.shape, low_ref.dtype)
    for f in range(blocks.shape[0]):
        row = rows[0, f]

        @pl.when((f < count[0]) & (row >= first) & (row < last))
        def _():
            high, low = split(blocks[f])
            at_row = pl.ds(pl.multiple_of((row - first) * order, order), order)
            at_col = pl.ds(pl.multiple_of(cols[0, f] * order, order), order)
            high_ref[at_row, at_col] = high
            low_ref[at_row, at_col] = low


def border_kernel(
    count, rows_in, cols_in, occ, virt, blocks, out, high_out, low_out, blocks_buf,
    rows, cols, occ_buf, virt_buf, fit_high, fit_low, sems,
):
    points = occ.shape[-1]
    step = points // CHUNKS
    first = [
        pltpu.make_async_copy(src, dst, sems.at[2 * CHUNKS + i])
        for i, (src, dst) in enumerate(
            ((rows_in, rows), (cols_in, cols), (blocks.at[0], blocks_buf))
        )
    ]
    for fetch in first:
        fetch.start()
    fetches = []
    for c in range(CHUNKS):
        at = slice(c * step, (c + 1) * step)
        fetches.append(
            [
                pltpu.make_async_copy(src.at[0, 0, at], dst.at[at], sems.at[2 * c + i])
                for i, (src, dst) in enumerate(((occ, occ_buf), (virt, virt_buf)))
            ]
        )
        for fetch in fetches[c]:
            fetch.start()
    for fetch in first:
        fetch.wait()
    place_fit(rows, cols, count, blocks_buf, fit_high, fit_low, OWN_BLK, OWN_BLK + BORDER_BLK)
    left = None
    for c in range(CHUNKS):
        at = slice(c * step, (c + 1) * step)
        for fetch in fetches[c]:
            fetch.wait()
        product = split(occ_buf[at] * virt_buf[at])
        high_out[at], low_out[at] = product
        term = dot3((fit_high[:, at], fit_low[:, at]), product, NN)
        left = term if left is None else left + term
    out[...] = dot3_halves(split(left), (fit_high[...], fit_low[...]), NT)


def own_kernel(
    rows, cols, count, border_map, pairs, cosine, product_high, product_low, blocks, metric,
    out, row_high, row_low, col_high, col_low, weight,
    fit_high, fit_low, proj_high, proj_low, pick_high, pick_low, edge,
):
    order = blocks.shape[-1]
    place_fit(rows, cols, count, blocks, fit_high, fit_low, 0, OWN_BLK)
    for j in range(BORDER_BLK):
        at = pl.ds(pl.multiple_of(border_map[0, j] * order, order), order)
        edge[:, j * order : (j + 1) * order] = metric[:, at]
    high, low = split(dot3(split(metric[...]), (fit_high[...], fit_low[...]), NN))
    proj_high[...] = high
    proj_low[...] = low
    count_pairs = out.shape[0]
    for p in range(count_pairs):
        here = slice(p * order, (p + 1) * order)
        at = pl.ds(pl.multiple_of(pairs[0, 0, p] * order, order), order)
        pick_high[here, :] = proj_high[at, :]
        pick_low[here, :] = proj_low[at, :]
        row_high[here, :], row_low[here, :] = split(edge[at, :])
        at = pl.ds(pl.multiple_of(pairs[0, 1, p] * order, order), order)
        col_high[here, :], col_low[here, :] = split(edge[at, :])
    left = dot3(
        (pick_high[...], pick_low[...]), (product_high[...], product_low[...]), NN
    )
    for p in range(count_pairs):
        at = pl.ds(pl.multiple_of(pairs[0, 1, p] * order, order), order)
        out[p] = dot3(
            split(left[p * order : (p + 1) * order, :]), (proj_high[at, :], proj_low[at, :]), NT
        )
    index = lax.axis_index("tm")
    chip, core = index // CORES, index % CORES
    chips = weight.shape[0]
    for k in range(chips):
        freq = to_chip(1, chip, k, chips) * CORES + core
        for j in range(chips):
            at = from_chip(0, chip, j, chips) * CORES
            weight[k, j, 0] = jnp.full(weight.shape[3:], cosine[freq, at + core])
            weight[k, j, 1] = jnp.full(weight.shape[3:], cosine[freq, at + 1 - core])


def join_kernel(border, own, row_high, row_low, col_high, col_low, *refs):
    total, outs = refs[-1], refs[:-1]
    chip = lax.axis_index("tm") // CORES
    count_pairs, order, _ = own.shape
    left = dot3_halves((row_high[...], row_low[...]), split(border[...]), NN)
    for p in range(count_pairs):
        here = slice(p * order, (p + 1) * order)
        total[p] = own[p] + dot3(split(left[here]), (col_high[here], col_low[here]), NT)
    share = outs[0].shape[1]
    for k, out in enumerate(outs):
        at = pl.ds(pl.multiple_of(to_chip(0, chip, k, len(outs)) * share, share), share)
        out[...] = total[:, at, :]


def combine_kernel(weight, *refs):
    chips = len(refs) // 3
    mine, other, outs = refs[:chips], refs[chips : 2 * chips], refs[2 * chips :]
    for k in range(chips):
        total = jnp.zeros(outs[k].shape, jnp.float32)
        for j in range(chips):
            total += weight[k, j, 0] * mine[j][...]
            total += weight[k, j, 1] * other[j][...]
        outs[k][...] = total


def gather_kernel(*refs):
    parts, out, sems = refs[:-2], refs[-2], refs[-1]
    chip = lax.axis_index("tm") // CORES
    copies = []
    for k, part in enumerate(parts):
        share = part.shape[1]
        at = pl.ds(pl.multiple_of(from_chip(1, chip, k, len(parts)) * share, share), share)
        copies.append(pltpu.make_async_copy(part, out.at[0, 0, :, at, :], sems.at[k]))
        copies[k].start()
    for copy in copies:
        copy.wait()


def in_vmem(x):
    return pltpu.with_memory_space_constraint(x, pltpu.VMEM)


def in_hbm(x):
    return pltpu.with_memory_space_constraint(x, pltpu.HBM)


def on_device(
    green_occ,
    virtual_green_time,
    fit_rows,
    fit_cols,
    fit_count,
    fit_blocks,
    border_map,
    coulomb_metric_root,
    pair_list,
    times,
    time_weights,
    freqs,
):
    points = green_occ.shape[-1]
    order = fit_blocks.shape[-1]
    own_rows = OWN_BLK * order
    edge_rows = BORDER_BLK * order
    pairs = pair_list.shape[1]
    devices = lax.axis_size("tm")
    chips = devices // CORES
    share = order // chips
    f32, bf16 = jnp.float32, jnp.bfloat16
    cosine = time_weights[None, :] * jnp.cos(freqs[:, None] * times[None, :])
    pair_rows_cols = jnp.swapaxes(pair_list, 1, 2)
    limit = pltpu.CompilerParams(vmem_limit_bytes=VMEM_LIMIT)

    border, product_high, product_low, blocks = pl.pallas_call(
        border_kernel,
        out_shape=(
            pltpu.VMEM((edge_rows, edge_rows), f32),
            pltpu.VMEM((points, points), bf16),
            pltpu.VMEM((points, points), bf16),
            pltpu.VMEM(fit_blocks.shape[1:], f32),
        ),
        in_specs=[SMEM] + [HBM] * 5,
        out_specs=(VMEM,) * 4,
        scratch_shapes=[pltpu.SMEM(fit_rows.shape, jnp.int32)] * 2
        + [pltpu.VMEM((points, points), f32)] * 2
        + [pltpu.VMEM((edge_rows, points), bf16)] * 2
        + [pltpu.SemaphoreType.DMA((2 * CHUNKS + 3,))],
        cost_estimate=pl.CostEstimate(flops=10**9, bytes_accessed=3 << 20, transcendentals=0),
        compiler_params=limit,
        name="border",
    )(
        fit_count, in_hbm(fit_rows), in_hbm(fit_cols),
        in_hbm(green_occ), in_hbm(virtual_green_time), in_hbm(fit_blocks),
    )
    sections = lax.axis_size("sec")
    border = lax.ppermute(border, "sec", [(i, (i + 1) % sections) for i in range(sections)])

    edge = pltpu.VMEM((pairs * order, edge_rows), bf16)
    own, row_high, row_low, col_high, col_low, weight = pl.pallas_call(
        own_kernel,
        out_shape=(pltpu.VMEM((pairs, order, order), f32),)
        + (edge,) * 4
        + (pltpu.VMEM((chips, chips, CORES, SUBLANES, order), f32),),
        in_specs=[SMEM] * 6 + [VMEM] * 4,
        out_specs=(VMEM,) * 6,
        scratch_shapes=[pltpu.VMEM((own_rows, points), bf16)] * 4
        + [pltpu.VMEM((pairs * order, points), bf16)] * 2
        + [pltpu.VMEM((own_rows, edge_rows), f32)],
        cost_estimate=pl.CostEstimate(flops=2 * 10**9, bytes_accessed=5 << 20, transcendentals=0),
        compiler_params=limit,
        name="own",
    )(
        fit_rows, fit_cols, fit_count, border_map, pair_rows_cols, cosine,
        in_vmem(product_high), in_vmem(product_low),
        in_vmem(blocks), in_hbm(coulomb_metric_root[0]),
    )

    part = pltpu.VMEM((pairs, share, order), f32)
    parts = pl.pallas_call(
        join_kernel,
        out_shape=(part,) * chips,
        in_specs=[VMEM] * 6,
        out_specs=(VMEM,) * chips,
        scratch_shapes=[pltpu.VMEM((pairs, order, order), f32)],
        compiler_params=limit,
        name="join",
    )(*map(in_vmem, (border, own, row_high, row_low, col_high, col_low)))

    def across(x, k, phase):
        pairs_of = [
            (i, to_chip(phase, i // CORES, k, chips) * CORES + i % CORES) for i in range(devices)
        ]
        return lax.ppermute(x, "tm", pairs_of)

    def swap(x):
        return lax.ppermute(x, "tm", [(i, i ^ 1) for i in range(devices)])

    mine = [parts[0]] + [across(parts[k], k, 0) for k in range(1, chips)]
    other = [swap(x) for x in mine]
    tiles = pltpu.VMEM((pairs * share // SUBLANES, SUBLANES, order), f32)
    parts = pl.pallas_call(
        combine_kernel,
        out_shape=(tiles,) * chips,
        in_specs=[VMEM] * (2 * chips + 1),
        out_specs=(VMEM,) * chips,
        compiler_params=limit,
        name="combine",
    )(*(in_vmem(x.reshape(tiles.shape) if x.ndim == 3 else x) for x in (weight, *mine, *other)))
    parts = [x.reshape(part.shape) for x in parts]
    parts = [parts[0]] + [across(parts[k], k, 1) for k in range(1, chips)]
    return pl.pallas_call(
        gather_kernel,
        out_shape=jax.ShapeDtypeStruct((1, 1, pairs, order, order), f32),
        in_specs=[VMEM] * chips,
        out_specs=ANY,
        scratch_shapes=[pltpu.SemaphoreType.DMA((chips,))],
        compiler_params=limit,
        name="gather",
    )(*map(in_vmem, parts))


def solution(mesh):
    return jax.shard_map(
        on_device,
        mesh=mesh,
        in_specs=(
            P("tm", "sec", None, None),
            P("tm", "sec", None, None),
            P("sec", None),
            P("sec", None),
            P("sec"),
            P("sec", None, None, None),
            P("sec", None),
            P("sec", None, None),
            P("sec", None, None),
            P(),
            P(),
            P(),
        ),
        out_specs=P("tm", "sec", None, None, None),
        check_vma=False,
    )
```

```python
import functools

import jax
import jax.numpy as jnp
from jax import lax
from jax.experimental import pallas as pl
from jax.experimental.pallas import tpu as pltpu
from jax.sharding import PartitionSpec as P


OWN_BLK = 4
BORDER_BLK = 2
CORES = 2
SUBLANES = 8

VMEM = pl.BlockSpec(memory_space=pltpu.VMEM)
SMEM = pl.BlockSpec(memory_space=pltpu.SMEM)
ANY = pl.BlockSpec(memory_space=pl.ANY)
HBM = pl.BlockSpec(memory_space=pltpu.HBM)
CHUNKS = 2
VMEM_LIMIT = 16 << 20
PARTNERS = 2
NN = (((1,), (0,)), ((), ()))
NT = (((1,), (1,)), ((), ()))


def split(x):
    high = x.astype(jnp.bfloat16)
    return high, (x - high.astype(jnp.float32)).astype(jnp.bfloat16)


def dot3(a, b, dims):
    mm = functools.partial(
        lax.dot_general, dimension_numbers=dims, preferred_element_type=jnp.float32
    )
    return mm(a[0], b[0]) + (mm(a[0], b[1]) + mm(a[1], b[0]))


def dot3_halves(a, b, dims):
    half = a[0].shape[0] // 2
    return jnp.concatenate(
        [dot3((a[0][at], a[1][at]), b, dims) for at in (slice(0, half), slice(half, 2 * half))],
        axis=0,
    )


def place_fit(rows, cols, count, blocks, high_ref, low_ref, first, last):
    order = blocks.shape[-1]
    high_ref[...] = jnp.zeros(high_ref.shape, high_ref.dtype)
    low_ref[...] = jnp.zeros(low_ref.shape, low_ref.dtype)
    for f in range(blocks.shape[0]):
        row = rows[0, f]

        @pl.when((f < count[0]) & (row >= first) & (row < last))
        def _():
            high, low = split(blocks[f])
            at_row = pl.ds(pl.multiple_of((row - first) * order, order), order)
            at_col = pl.ds(pl.multiple_of(cols[0, f] * order, order), order)
            high_ref[at_row, at_col] = high
            low_ref[at_row, at_col] = low


def border_kernel(
    count, rows_in, cols_in, occ, virt, blocks, out, high_out, low_out, blocks_buf,
    rows, cols, occ_buf, virt_buf, fit_high, fit_low, sems,
):
    points = occ.shape[-1]
    step = points // CHUNKS
    first = [
        pltpu.make_async_copy(src, dst, sems.at[2 * CHUNKS + i])
        for i, (src, dst) in enumerate(
            ((rows_in, rows), (cols_in, cols), (blocks.at[0], blocks_buf))
        )
    ]
    for fetch in first:
        fetch.start()
    fetches = []
    for c in range(CHUNKS):
        at = slice(c * step, (c + 1) * step)
        fetches.append(
            [
                pltpu.make_async_copy(src.at[0, 0, at], dst.at[at], sems.at[2 * c + i])
                for i, (src, dst) in enumerate(((occ, occ_buf), (virt, virt_buf)))
            ]
        )
        for fetch in fetches[c]:
            fetch.start()
    for fetch in first:
        fetch.wait()
    place_fit(rows, cols, count, blocks_buf, fit_high, fit_low, OWN_BLK, OWN_BLK + BORDER_BLK)
    left = None
    for c in range(CHUNKS):
        at = slice(c * step, (c + 1) * step)
        for fetch in fetches[c]:
            fetch.wait()
        product = split(occ_buf[at] * virt_buf[at])
        high_out[at], low_out[at] = product
        term = dot3((fit_high[:, at], fit_low[:, at]), product, NN)
        left = term if left is None else left + term
    out[...] = dot3_halves(split(left), (fit_high[...], fit_low[...]), NT)


def own_kernel(
    rows, cols, count, border_map, pairs, cosine, product_high, product_low, blocks, metric,
    out, row_high, row_low, col_high, col_low, weight,
    fit_high, fit_low, proj_high, proj_low, pick_high, pick_low, edge,
):
    order = blocks.shape[-1]
    place_fit(rows, cols, count, blocks, fit_high, fit_low, 0, OWN_BLK)
    for j in range(BORDER_BLK):
        at = pl.ds(pl.multiple_of(border_map[0, j] * order, order), order)
        edge[:, j * order : (j + 1) * order] = metric[:, at]
    high, low = split(dot3(split(metric[...]), (fit_high[...], fit_low[...]), NN))
    proj_high[...] = high
    proj_low[...] = low
    count_pairs = out.shape[0]
    for p in range(count_pairs):
        here = slice(p * order, (p + 1) * order)
        at = pl.ds(pl.multiple_of(pairs[0, 0, p] * order, order), order)
        pick_high[here, :] = proj_high[at, :]
        pick_low[here, :] = proj_low[at, :]
        row_high[here, :], row_low[here, :] = split(edge[at, :])
        at = pl.ds(pl.multiple_of(pairs[0, 1, p] * order, order), order)
        col_high[here, :], col_low[here, :] = split(edge[at, :])
    left = dot3(
        (pick_high[...], pick_low[...]), (product_high[...], product_low[...]), NN
    )
    for p in range(count_pairs):
        at = pl.ds(pl.multiple_of(pairs[0, 1, p] * order, order), order)
        out[p] = dot3(
            split(left[p * order : (p + 1) * order, :]), (proj_high[at, :], proj_low[at, :]), NT
        )
    index = lax.axis_index("tm")
    chip, core = index // CORES, index % CORES
    chips = weight.shape[1]
    for k in range(PARTNERS):
        freq = (chip ^ k) * CORES + core
        for j in range(chips):
            at = (chip ^ j) * CORES
            weight[k, j, 0] = jnp.full(weight.shape[3:], cosine[freq, at + core])
            weight[k, j, 1] = jnp.full(weight.shape[3:], cosine[freq, at + 1 - core])


def join_kernel(border, own, row_high, row_low, col_high, col_low, *refs):
    total, outs = refs[-1], refs[:-1]
    chip = lax.axis_index("tm") // CORES
    count_pairs, order, _ = own.shape
    left = dot3_halves((row_high[...], row_low[...]), split(border[...]), NN)
    for p in range(count_pairs):
        here = slice(p * order, (p + 1) * order)
        total[p] = own[p] + dot3(split(left[here]), (col_high[here], col_low[here]), NT)
    share = outs[0].shape[1]
    for k, out in enumerate(outs):
        at = pl.ds(pl.multiple_of(((chip ^ k) % PARTNERS) * share, share), share)
        out[...] = total[:, at, :]


def combine_kernel(weight, *refs):
    chips = weight.shape[1]
    mine, other, outs = refs[:chips], refs[chips : 2 * chips], refs[2 * chips :]
    for k in range(PARTNERS):
        total = jnp.zeros(outs[k].shape, jnp.float32)
        for j in range(chips):
            total += weight[k, j, 0] * mine[j][...]
            total += weight[k, j, 1] * other[j][...]
        outs[k][...] = total


def gather_kernel(*refs):
    parts, out, sems = refs[:-2], refs[-2], refs[-1]
    chip = lax.axis_index("tm") // CORES
    copies = []
    for k, part in enumerate(parts):
        share = part.shape[1]
        at = pl.ds(pl.multiple_of(((chip ^ k) % PARTNERS) * share, share), share)
        copies.append(pltpu.make_async_copy(part, out.at[0, 0, :, at, :], sems.at[k]))
        copies[k].start()
    for copy in copies:
        copy.wait()


def in_vmem(x):
    return pltpu.with_memory_space_constraint(x, pltpu.VMEM)


def in_hbm(x):
    return pltpu.with_memory_space_constraint(x, pltpu.HBM)


def on_device(
    green_occ,
    virtual_green_time,
    fit_rows,
    fit_cols,
    fit_count,
    fit_blocks,
    border_map,
    coulomb_metric_root,
    pair_list,
    times,
    time_weights,
    freqs,
):
    points = green_occ.shape[-1]
    order = fit_blocks.shape[-1]
    own_rows = OWN_BLK * order
    edge_rows = BORDER_BLK * order
    pairs = pair_list.shape[1]
    devices = lax.axis_size("tm")
    chips = devices // CORES
    share = order // PARTNERS
    f32, bf16 = jnp.float32, jnp.bfloat16
    cosine = time_weights[None, :] * jnp.cos(freqs[:, None] * times[None, :])
    pair_rows_cols = jnp.swapaxes(pair_list, 1, 2)
    limit = pltpu.CompilerParams(vmem_limit_bytes=VMEM_LIMIT)

    border, product_high, product_low, blocks = pl.pallas_call(
        border_kernel,
        out_shape=(
            pltpu.VMEM((edge_rows, edge_rows), f32),
            pltpu.VMEM((points, points), bf16),
            pltpu.VMEM((points, points), bf16),
            pltpu.VMEM(fit_blocks.shape[1:], f32),
        ),
        in_specs=[SMEM] + [HBM] * 5,
        out_specs=(VMEM,) * 4,
        scratch_shapes=[pltpu.SMEM(fit_rows.shape, jnp.int32)] * 2
        + [pltpu.VMEM((points, points), f32)] * 2
        + [pltpu.VMEM((edge_rows, points), bf16)] * 2
        + [pltpu.SemaphoreType.DMA((2 * CHUNKS + 3,))],
        cost_estimate=pl.CostEstimate(flops=10**9, bytes_accessed=3 << 20, transcendentals=0),
        compiler_params=limit,
        name="border",
    )(
        fit_count, in_hbm(fit_rows), in_hbm(fit_cols),
        in_hbm(green_occ), in_hbm(virtual_green_time), in_hbm(fit_blocks),
    )
    sections = lax.axis_size("sec")
    border = lax.ppermute(border, "sec", [(i, (i + 1) % sections) for i in range(sections)])

    edge = pltpu.VMEM((pairs * order, edge_rows), bf16)
    own, row_high, row_low, col_high, col_low, weight = pl.pallas_call(
        own_kernel,
        out_shape=(pltpu.VMEM((pairs, order, order), f32),)
        + (edge,) * 4
        + (pltpu.VMEM((PARTNERS, chips, CORES, SUBLANES, order), f32),),
        in_specs=[SMEM] * 6 + [VMEM] * 4,
        out_specs=(VMEM,) * 6,
        scratch_shapes=[pltpu.VMEM((own_rows, points), bf16)] * 4
        + [pltpu.VMEM((pairs * order, points), bf16)] * 2
        + [pltpu.VMEM((own_rows, edge_rows), f32)],
        cost_estimate=pl.CostEstimate(flops=2 * 10**9, bytes_accessed=5 << 20, transcendentals=0),
        compiler_params=limit,
        name="own",
    )(
        fit_rows, fit_cols, fit_count, border_map, pair_rows_cols, cosine,
        in_vmem(product_high), in_vmem(product_low),
        in_vmem(blocks), in_hbm(coulomb_metric_root[0]),
    )

    part = pltpu.VMEM((pairs, share, order), f32)
    parts = pl.pallas_call(
        join_kernel,
        out_shape=(part,) * PARTNERS,
        in_specs=[VMEM] * 6,
        out_specs=(VMEM,) * PARTNERS,
        scratch_shapes=[pltpu.VMEM((pairs, order, order), f32)],
        compiler_params=limit,
        name="join",
    )(*map(in_vmem, (border, own, row_high, row_low, col_high, col_low)))

    def across(x, k):
        pairs_of = [
            (i, i ^ (CORES * k)) for i in range(devices)
        ]
        return lax.ppermute(x, "tm", pairs_of)

    def swap(x):
        return lax.ppermute(x, "tm", [(i, i ^ 1) for i in range(devices)])

    mine = [parts[0]] + [across(parts[k % PARTNERS], k) for k in range(1, chips)]
    other = [swap(x) for x in mine]
    tiles = pltpu.VMEM((pairs * share // SUBLANES, SUBLANES, order), f32)
    parts = pl.pallas_call(
        combine_kernel,
        out_shape=(tiles,) * PARTNERS,
        in_specs=[VMEM] * (2 * chips + 1),
        out_specs=(VMEM,) * PARTNERS,
        compiler_params=limit,
        name="combine",
    )(*(in_vmem(x.reshape(tiles.shape) if x.ndim == 3 else x) for x in (weight, *mine, *other)))
    parts = [x.reshape(part.shape) for x in parts]
    parts = [parts[0]] + [across(parts[k], k) for k in range(1, PARTNERS)]
    return pl.pallas_call(
        gather_kernel,
        out_shape=jax.ShapeDtypeStruct((1, 1, pairs, order, order), f32),
        in_specs=[VMEM] * PARTNERS,
        out_specs=ANY,
        scratch_shapes=[pltpu.SemaphoreType.DMA((PARTNERS,))],
        compiler_params=limit,
        name="gather",
    )(*map(in_vmem, parts))


def solution(mesh):
    return jax.shard_map(
        on_device,
        mesh=mesh,
        in_specs=(
            P("tm", "sec", None, None),
            P("tm", "sec", None, None),
            P("sec", None),
            P("sec", None),
            P("sec"),
            P("sec", None, None, None),
            P("sec", None),
            P("sec", None, None),
            P("sec", None, None),
            P(),
            P(),
            P(),
        ),
        out_specs=P("tm", "sec", None, None, None),
        check_vma=False,
    )
```

```python
import functools

import jax
import jax.numpy as jnp
from jax import lax
from jax.experimental import pallas as pl
from jax.experimental.pallas import tpu as pltpu
from jax.sharding import PartitionSpec as P


OWN_BLK = 4
BORDER_BLK = 2
CORES = 2
SUBLANES = 8

VMEM = pl.BlockSpec(memory_space=pltpu.VMEM)
SMEM = pl.BlockSpec(memory_space=pltpu.SMEM)
ANY = pl.BlockSpec(memory_space=pl.ANY)
HBM = pl.BlockSpec(memory_space=pltpu.HBM)
CHUNKS = 2
VMEM_LIMIT = 16 << 20
PARTNERS = 2
NN = (((1,), (0,)), ((), ()))
NT = (((1,), (1,)), ((), ()))


def split(x):
    high = x.astype(jnp.bfloat16)
    return high, (x - high.astype(jnp.float32)).astype(jnp.bfloat16)


def dot3(a, b, dims):
    mm = functools.partial(
        lax.dot_general, dimension_numbers=dims, preferred_element_type=jnp.float32
    )
    return mm(a[0], b[0]) + (mm(a[0], b[1]) + mm(a[1], b[0]))


def dot3_halves(a, b, dims):
    half = a[0].shape[0] // 2
    return jnp.concatenate(
        [dot3((a[0][at], a[1][at]), b, dims) for at in (slice(0, half), slice(half, 2 * half))],
        axis=0,
    )


def place_fit(rows, cols, count, blocks, high_ref, low_ref, first, last):
    order = blocks.shape[-1]
    high_ref[...] = jnp.zeros(high_ref.shape, high_ref.dtype)
    low_ref[...] = jnp.zeros(low_ref.shape, low_ref.dtype)
    for f in range(blocks.shape[0]):
        row = rows[0, f]

        @pl.when((f < count[0]) & (row >= first) & (row < last))
        def _():
            high, low = split(blocks[f])
            at_row = pl.ds(pl.multiple_of((row - first) * order, order), order)
            at_col = pl.ds(pl.multiple_of(cols[0, f] * order, order), order)
            high_ref[at_row, at_col] = high
            low_ref[at_row, at_col] = low


def border_kernel(
    count, rows_in, cols_in, occ, virt, blocks, out, high_out, low_out, blocks_buf,
    rows, cols, occ_buf, virt_buf, fit_high, fit_low, sems,
):
    points = occ.shape[-1]
    step = points // CHUNKS
    first = [
        pltpu.make_async_copy(src, dst, sems.at[2 * CHUNKS + i])
        for i, (src, dst) in enumerate(
            ((rows_in, rows), (cols_in, cols), (blocks.at[0], blocks_buf))
        )
    ]
    for fetch in first:
        fetch.start()
    fetches = []
    for c in range(CHUNKS):
        at = slice(c * step, (c + 1) * step)
        fetches.append(
            [
                pltpu.make_async_copy(src.at[0, 0, at], dst.at[at], sems.at[2 * c + i])
                for i, (src, dst) in enumerate(((occ, occ_buf), (virt, virt_buf)))
            ]
        )
        for fetch in fetches[c]:
            fetch.start()
    for fetch in first:
        fetch.wait()
    place_fit(rows, cols, count, blocks_buf, fit_high, fit_low, OWN_BLK, OWN_BLK + BORDER_BLK)
    left = None
    for c in range(CHUNKS):
        at = slice(c * step, (c + 1) * step)
        for fetch in fetches[c]:
            fetch.wait()
        product = split(occ_buf[at] * virt_buf[at])
        high_out[at], low_out[at] = product
        term = dot3((fit_high[:, at], fit_low[:, at]), product, NN)
        left = term if left is None else left + term
    left = split(left)
    half = out.shape[1] // 2
    for at in (slice(0, half), slice(half, 2 * half)):
        out[:, at] = dot3(left, (fit_high[at, :], fit_low[at, :]), NT)


def own_kernel(
    rows, cols, count, border_map, pairs, cosine, product_high, product_low, blocks, metric,
    out, row_high, row_low, col_high, col_low, weight,
    fit_high, fit_low, proj_high, proj_low, pick_high, pick_low, edge,
):
    order = blocks.shape[-1]
    place_fit(rows, cols, count, blocks, fit_high, fit_low, 0, OWN_BLK)
    for j in range(BORDER_BLK):
        at = pl.ds(pl.multiple_of(border_map[0, j] * order, order), order)
        edge[:, j * order : (j + 1) * order] = metric[:, at]
    high, low = split(dot3(split(metric[...]), (fit_high[...], fit_low[...]), NN))
    proj_high[...] = high
    proj_low[...] = low
    count_pairs = out.shape[0]
    for p in range(count_pairs):
        here = slice(p * order, (p + 1) * order)
        at = pl.ds(pl.multiple_of(pairs[0, 0, p] * order, order), order)
        pick_high[here, :] = proj_high[at, :]
        pick_low[here, :] = proj_low[at, :]
        row_high[here, :], row_low[here, :] = split(edge[at, :])
        at = pl.ds(pl.multiple_of(pairs[0, 1, p] * order, order), order)
        col_high[here, :], col_low[here, :] = split(edge[at, :])
    left = dot3(
        (pick_high[...], pick_low[...]), (product_high[...], product_low[...]), NN
    )
    for p in range(count_pairs):
        at = pl.ds(pl.multiple_of(pairs[0, 1, p] * order, order), order)
        out[p] = dot3(
            split(left[p * order : (p + 1) * order, :]), (proj_high[at, :], proj_low[at, :]), NT
        )
    index = lax.axis_index("tm")
    chip, core = index // CORES, index % CORES
    chips = weight.shape[1]
    for k in range(PARTNERS):
        freq = (chip ^ k) * CORES + core
        for j in range(chips):
            at = (chip ^ j) * CORES
            weight[k, j, 0] = jnp.full(weight.shape[3:], cosine[freq, at + core])
            weight[k, j, 1] = jnp.full(weight.shape[3:], cosine[freq, at + 1 - core])


def join_kernel(border, own, row_high, row_low, col_high, col_low, *refs):
    total, outs = refs[-1], refs[:-1]
    chip = lax.axis_index("tm") // CORES
    count_pairs, order, _ = own.shape
    left = dot3_halves((row_high[...], row_low[...]), split(border[...]), NN)
    for p in range(count_pairs):
        here = slice(p * order, (p + 1) * order)
        total[p] = own[p] + dot3(split(left[here]), (col_high[here], col_low[here]), NT)
    share = outs[0].shape[1]
    for k, out in enumerate(outs):
        at = pl.ds(pl.multiple_of(((chip ^ k) % PARTNERS) * share, share), share)
        out[...] = total[:, at, :]


def combine_kernel(weight, *refs):
    chips = weight.shape[1]
    mine, other, outs = refs[:chips], refs[chips : 2 * chips], refs[2 * chips :]
    for k in range(PARTNERS):
        total = jnp.zeros(outs[k].shape, jnp.float32)
        for j in range(chips):
            total += weight[k, j, 0] * mine[j][...]
            total += weight[k, j, 1] * other[j][...]
        outs[k][...] = total


def gather_kernel(*refs):
    parts, out, sems = refs[:-2], refs[-2], refs[-1]
    chip = lax.axis_index("tm") // CORES
    copies = []
    for k, part in enumerate(parts):
        share = part.shape[1]
        at = pl.ds(pl.multiple_of(((chip ^ k) % PARTNERS) * share, share), share)
        for p in range(part.shape[0]):
            copies.append(pltpu.make_async_copy(part.at[p], out.at[0, 0, p, at, :], sems.at[k, p]))
            copies[-1].start()
    for copy in copies:
        copy.wait()


def in_vmem(x):
    return pltpu.with_memory_space_constraint(x, pltpu.VMEM)


def in_hbm(x):
    return pltpu.with_memory_space_constraint(x, pltpu.HBM)


def on_device(
    green_occ,
    virtual_green_time,
    fit_rows,
    fit_cols,
    fit_count,
    fit_blocks,
    border_map,
    coulomb_metric_root,
    pair_list,
    times,
    time_weights,
    freqs,
):
    points = green_occ.shape[-1]
    order = fit_blocks.shape[-1]
    own_rows = OWN_BLK * order
    edge_rows = BORDER_BLK * order
    pairs = pair_list.shape[1]
    devices = lax.axis_size("tm")
    chips = devices // CORES
    share = order // PARTNERS
    f32, bf16 = jnp.float32, jnp.bfloat16
    cosine = time_weights[None, :] * jnp.cos(freqs[:, None] * times[None, :])
    pair_rows_cols = jnp.swapaxes(pair_list, 1, 2)
    limit = pltpu.CompilerParams(vmem_limit_bytes=VMEM_LIMIT)

    border, product_high, product_low, blocks = pl.pallas_call(
        border_kernel,
        out_shape=(
            pltpu.VMEM((edge_rows, edge_rows), f32),
            pltpu.VMEM((points, points), bf16),
            pltpu.VMEM((points, points), bf16),
            pltpu.VMEM(fit_blocks.shape[1:], f32),
        ),
        in_specs=[SMEM] + [HBM] * 5,
        out_specs=(VMEM,) * 4,
        scratch_shapes=[pltpu.SMEM(fit_rows.shape, jnp.int32)] * 2
        + [pltpu.VMEM((points, points), f32)] * 2
        + [pltpu.VMEM((edge_rows, points), bf16)] * 2
        + [pltpu.SemaphoreType.DMA((2 * CHUNKS + 3,))],
        cost_estimate=pl.CostEstimate(flops=10**9, bytes_accessed=3 << 20, transcendentals=0),
        compiler_params=limit,
        name="border",
    )(
        fit_count, in_hbm(fit_rows), in_hbm(fit_cols),
        in_hbm(green_occ), in_hbm(virtual_green_time), in_hbm(fit_blocks),
    )
    sections = lax.axis_size("sec")
    border = lax.ppermute(border, "sec", [(i, (i + 1) % sections) for i in range(sections)])

    edge = pltpu.VMEM((pairs * order, edge_rows), bf16)
    own, row_high, row_low, col_high, col_low, weight = pl.pallas_call(
        own_kernel,
        out_shape=(pltpu.VMEM((pairs, order, order), f32),)
        + (edge,) * 4
        + (pltpu.VMEM((PARTNERS, chips, CORES, SUBLANES, order), f32),),
        in_specs=[SMEM] * 6 + [VMEM] * 4,
        out_specs=(VMEM,) * 6,
        scratch_shapes=[pltpu.VMEM((own_rows, points), bf16)] * 4
        + [pltpu.VMEM((pairs * order, points), bf16)] * 2
        + [pltpu.VMEM((own_rows, edge_rows), f32)],
        cost_estimate=pl.CostEstimate(flops=2 * 10**9, bytes_accessed=5 << 20, transcendentals=0),
        compiler_params=limit,
        name="own",
    )(
        fit_rows, fit_cols, fit_count, border_map, pair_rows_cols, cosine,
        in_vmem(product_high), in_vmem(product_low),
        in_vmem(blocks), in_hbm(coulomb_metric_root[0]),
    )

    part = pltpu.VMEM((pairs, share, order), f32)
    parts = pl.pallas_call(
        join_kernel,
        out_shape=(part,) * PARTNERS,
        in_specs=[VMEM] * 6,
        out_specs=(VMEM,) * PARTNERS,
        scratch_shapes=[pltpu.VMEM((pairs, order, order), f32)],
        compiler_params=limit,
        name="join",
    )(*map(in_vmem, (border, own, row_high, row_low, col_high, col_low)))

    def across(x, k):
        pairs_of = [
            (i, i ^ (CORES * k)) for i in range(devices)
        ]
        return lax.ppermute(x, "tm", pairs_of)

    def swap(x):
        return lax.ppermute(x, "tm", [(i, i ^ 1) for i in range(devices)])

    mine = [parts[0]] + [across(parts[k % PARTNERS], k) for k in range(1, chips)]
    other = [swap(x) for x in mine]
    tiles = pltpu.VMEM((pairs * share // SUBLANES, SUBLANES, order), f32)
    parts = pl.pallas_call(
        combine_kernel,
        out_shape=(tiles,) * PARTNERS,
        in_specs=[VMEM] * (2 * chips + 1),
        out_specs=(VMEM,) * PARTNERS,
        compiler_params=limit,
        name="combine",
    )(*(in_vmem(x.reshape(tiles.shape) if x.ndim == 3 else x) for x in (weight, *mine, *other)))
    parts = [x.reshape(part.shape) for x in parts]
    parts = [parts[0]] + [across(parts[k], k) for k in range(1, PARTNERS)]
    return pl.pallas_call(
        gather_kernel,
        out_shape=jax.ShapeDtypeStruct((1, 1, pairs, order, order), f32),
        in_specs=[VMEM] * PARTNERS,
        out_specs=ANY,
        scratch_shapes=[pltpu.SemaphoreType.DMA((PARTNERS, pairs))],
        compiler_params=limit,
        name="gather",
    )(*map(in_vmem, parts))


def solution(mesh):
    return jax.shard_map(
        on_device,
        mesh=mesh,
        in_specs=(
            P("tm", "sec", None, None),
            P("tm", "sec", None, None),
            P("sec", None),
            P("sec", None),
            P("sec"),
            P("sec", None, None, None),
            P("sec", None),
            P("sec", None, None),
            P("sec", None, None),
            P(),
            P(),
            P(),
        ),
        out_specs=P("tm", "sec", None, None, None),
        check_vma=False,
    )
```

```python
import functools

import jax
import jax.numpy as jnp
from jax import lax
from jax.experimental import pallas as pl
from jax.experimental.pallas import tpu as pltpu
from jax.sharding import PartitionSpec as P


OWN_BLK = 4
BORDER_BLK = 2
CORES = 2
SUBLANES = 8

VMEM = pl.BlockSpec(memory_space=pltpu.VMEM)
SMEM = pl.BlockSpec(memory_space=pltpu.SMEM)
ANY = pl.BlockSpec(memory_space=pl.ANY)
HBM = pl.BlockSpec(memory_space=pltpu.HBM)
CHUNKS = 2
VMEM_LIMIT = 16 << 20
PARTNERS = 2
NN = (((1,), (0,)), ((), ()))
NT = (((1,), (1,)), ((), ()))


def split(x):
    high = x.astype(jnp.bfloat16)
    return high, (x - high.astype(jnp.float32)).astype(jnp.bfloat16)


def dot3(a, b, dims):
    mm = functools.partial(
        lax.dot_general, dimension_numbers=dims, preferred_element_type=jnp.float32
    )
    return mm(a[0], b[0]) + (mm(a[0], b[1]) + mm(a[1], b[0]))


def dot3_halves(a, b, dims):
    half = a[0].shape[0] // 2
    return jnp.concatenate(
        [dot3((a[0][at], a[1][at]), b, dims) for at in (slice(0, half), slice(half, 2 * half))],
        axis=0,
    )


def place_fit(rows, cols, count, blocks, high_ref, low_ref, first, last):
    order = blocks.shape[-1]
    high_ref[...] = jnp.zeros(high_ref.shape, high_ref.dtype)
    low_ref[...] = jnp.zeros(low_ref.shape, low_ref.dtype)
    for f in range(blocks.shape[0]):
        row = rows[0, f]

        @pl.when((f < count[0]) & (row >= first) & (row < last))
        def _():
            high, low = split(blocks[f])
            at_row = pl.ds(pl.multiple_of((row - first) * order, order), order)
            at_col = pl.ds(pl.multiple_of(cols[0, f] * order, order), order)
            high_ref[at_row, at_col] = high
            low_ref[at_row, at_col] = low


def border_kernel(
    count, rows_in, cols_in, occ, virt, blocks, out, high_out, low_out, blocks_buf,
    rows, cols, occ_buf, virt_buf, fit_high, fit_low, sems,
):
    points = occ.shape[-1]
    step = points // CHUNKS
    first = [
        pltpu.make_async_copy(src, dst, sems.at[2 * CHUNKS + i])
        for i, (src, dst) in enumerate(
            ((rows_in, rows), (cols_in, cols), (blocks.at[0], blocks_buf))
        )
    ]
    for fetch in first:
        fetch.start()
    fetches = []
    for c in range(CHUNKS):
        at = slice(c * step, (c + 1) * step)
        fetches.append(
            [
                pltpu.make_async_copy(src.at[0, 0, at], dst.at[at], sems.at[2 * c + i])
                for i, (src, dst) in enumerate(((occ, occ_buf), (virt, virt_buf)))
            ]
        )
        for fetch in fetches[c]:
            fetch.start()
    for fetch in first:
        fetch.wait()
    place_fit(rows, cols, count, blocks_buf, fit_high, fit_low, OWN_BLK, OWN_BLK + BORDER_BLK)
    left = None
    for c in range(CHUNKS):
        at = slice(c * step, (c + 1) * step)
        for fetch in fetches[c]:
            fetch.wait()
        product = split(occ_buf[at] * virt_buf[at])
        high_out[at], low_out[at] = product
        term = dot3((fit_high[:, at], fit_low[:, at]), product, NN)
        left = term if left is None else left + term
    out[...] = dot3_halves(split(left), (fit_high[...], fit_low[...]), NT)


def own_kernel(
    rows, cols, count, border_map, pairs, cosine, product_high, product_low, blocks, metric,
    out, row_high, row_low, col_high, col_low, weight,
    fit_high, fit_low, proj_high, proj_low, pick_high, pick_low, edge,
):
    order = blocks.shape[-1]
    place_fit(rows, cols, count, blocks, fit_high, fit_low, 0, OWN_BLK)
    for j in range(BORDER_BLK):
        at = pl.ds(pl.multiple_of(border_map[0, j] * order, order), order)
        edge[:, j * order : (j + 1) * order] = metric[:, at]
    high, low = split(dot3(split(metric[...]), (fit_high[...], fit_low[...]), NN))
    proj_high[...] = high
    proj_low[...] = low
    count_pairs = out.shape[0]
    for p in range(count_pairs):
        here = slice(p * order, (p + 1) * order)
        at = pl.ds(pl.multiple_of(pairs[0, 0, p] * order, order), order)
        pick_high[here, :] = proj_high[at, :]
        pick_low[here, :] = proj_low[at, :]
        row_high[here, :], row_low[here, :] = split(edge[at, :])
        at = pl.ds(pl.multiple_of(pairs[0, 1, p] * order, order), order)
        col_high[here, :], col_low[here, :] = split(edge[at, :])
    left = dot3(
        (pick_high[...], pick_low[...]), (product_high[...], product_low[...]), NN
    )
    for p in range(count_pairs):
        at = pl.ds(pl.multiple_of(pairs[0, 1, p] * order, order), order)
        out[p] = dot3(
            split(left[p * order : (p + 1) * order, :]), (proj_high[at, :], proj_low[at, :]), NT
        )
    index = lax.axis_index("tm")
    chip, core = index // CORES, index % CORES
    for k in range(PARTNERS):
        for d in range(CORES):
            freq = (chip ^ k) * CORES + (core ^ d)
            for j in range(weight.shape[2]):
                value = cosine[freq, (chip ^ j) * CORES + core]
                weight[k, d, j] = jnp.full(weight.shape[3:], value)


def join_kernel(border, own, row_high, row_low, col_high, col_low, *refs):
    total, outs = refs[-1], refs[:-1]
    chip = lax.axis_index("tm") // CORES
    count_pairs, order, _ = own.shape
    left = dot3_halves((row_high[...], row_low[...]), split(border[...]), NN)
    for p in range(count_pairs):
        here = slice(p * order, (p + 1) * order)
        total[p] = own[p] + dot3(split(left[here]), (col_high[here], col_low[here]), NT)
    share = outs[0].shape[1]
    for k, out in enumerate(outs):
        at = pl.ds(pl.multiple_of(((chip ^ k) % PARTNERS) * share, share), share)
        out[...] = total[:, at, :]


def combine_kernel(weight, *refs):
    chips = weight.shape[2]
    mine, outs = refs[:chips], refs[chips:]
    for q, out in enumerate(outs):
        total = jnp.zeros(out.shape, jnp.float32)
        for j in range(chips):
            total += weight[q // CORES, q % CORES, j] * mine[j][...]
        out[...] = total


def gather_kernel(*refs):
    parts, out = refs[:-1], refs[-1]
    chip = lax.axis_index("tm") // CORES
    share = parts[0].shape[1]
    for k in range(PARTNERS):
        at = pl.ds(pl.multiple_of(((chip ^ k) % PARTNERS) * share, share), share)
        out[0, 0, :, at, :] = parts[k * CORES][...] + parts[k * CORES + 1][...]


def in_vmem(x):
    return pltpu.with_memory_space_constraint(x, pltpu.VMEM)


def in_hbm(x):
    return pltpu.with_memory_space_constraint(x, pltpu.HBM)


def on_device(
    green_occ,
    virtual_green_time,
    fit_rows,
    fit_cols,
    fit_count,
    fit_blocks,
    border_map,
    coulomb_metric_root,
    pair_list,
    times,
    time_weights,
    freqs,
):
    points = green_occ.shape[-1]
    order = fit_blocks.shape[-1]
    own_rows = OWN_BLK * order
    edge_rows = BORDER_BLK * order
    pairs = pair_list.shape[1]
    devices = lax.axis_size("tm")
    chips = devices // CORES
    share = order // PARTNERS
    f32, bf16 = jnp.float32, jnp.bfloat16
    cosine = time_weights[None, :] * jnp.cos(freqs[:, None] * times[None, :])
    pair_rows_cols = jnp.swapaxes(pair_list, 1, 2)
    limit = pltpu.CompilerParams(vmem_limit_bytes=VMEM_LIMIT)

    border, product_high, product_low, blocks = pl.pallas_call(
        border_kernel,
        out_shape=(
            pltpu.VMEM((edge_rows, edge_rows), f32),
            pltpu.VMEM((points, points), bf16),
            pltpu.VMEM((points, points), bf16),
            pltpu.VMEM(fit_blocks.shape[1:], f32),
        ),
        in_specs=[SMEM] + [HBM] * 5,
        out_specs=(VMEM,) * 4,
        scratch_shapes=[pltpu.SMEM(fit_rows.shape, jnp.int32)] * 2
        + [pltpu.VMEM((points, points), f32)] * 2
        + [pltpu.VMEM((edge_rows, points), bf16)] * 2
        + [pltpu.SemaphoreType.DMA((2 * CHUNKS + 3,))],
        cost_estimate=pl.CostEstimate(flops=10**9, bytes_accessed=3 << 20, transcendentals=0),
        compiler_params=limit,
        name="border",
    )(
        fit_count, in_hbm(fit_rows), in_hbm(fit_cols),
        in_hbm(green_occ), in_hbm(virtual_green_time), in_hbm(fit_blocks),
    )
    sections = lax.axis_size("sec")
    border = lax.ppermute(border, "sec", [(i, (i + 1) % sections) for i in range(sections)])

    edge = pltpu.VMEM((pairs * order, edge_rows), bf16)
    own, row_high, row_low, col_high, col_low, weight = pl.pallas_call(
        own_kernel,
        out_shape=(pltpu.VMEM((pairs, order, order), f32),)
        + (edge,) * 4
        + (pltpu.VMEM((PARTNERS, CORES, chips, SUBLANES, order), f32),),
        in_specs=[SMEM] * 6 + [VMEM] * 4,
        out_specs=(VMEM,) * 6,
        scratch_shapes=[pltpu.VMEM((own_rows, points), bf16)] * 4
        + [pltpu.VMEM((pairs * order, points), bf16)] * 2
        + [pltpu.VMEM((own_rows, edge_rows), f32)],
        cost_estimate=pl.CostEstimate(flops=2 * 10**9, bytes_accessed=5 << 20, transcendentals=0),
        compiler_params=limit,
        name="own",
    )(
        fit_rows, fit_cols, fit_count, border_map, pair_rows_cols, cosine,
        in_vmem(product_high), in_vmem(product_low),
        in_vmem(blocks), in_hbm(coulomb_metric_root[0]),
    )

    part = pltpu.VMEM((pairs, share, order), f32)
    parts = pl.pallas_call(
        join_kernel,
        out_shape=(part,) * PARTNERS,
        in_specs=[VMEM] * 6,
        out_specs=(VMEM,) * PARTNERS,
        scratch_shapes=[pltpu.VMEM((pairs, order, order), f32)],
        compiler_params=limit,
        name="join",
    )(*map(in_vmem, (border, own, row_high, row_low, col_high, col_low)))

    def across(x, k):
        pairs_of = [
            (i, i ^ (CORES * k)) for i in range(devices)
        ]
        return lax.ppermute(x, "tm", pairs_of)

    def onward(x, k, d):
        return lax.ppermute(x, "tm", [(i, i ^ (CORES * k + d)) for i in range(devices)])

    mine = [parts[0]] + [across(parts[k % PARTNERS], k) for k in range(1, chips)]
    tiles = pltpu.VMEM((pairs * share // SUBLANES, SUBLANES, order), f32)
    sums = pl.pallas_call(
        combine_kernel,
        out_shape=(tiles,) * (PARTNERS * CORES),
        in_specs=[VMEM] * (chips + 1),
        out_specs=(VMEM,) * (PARTNERS * CORES),
        compiler_params=limit,
        name="combine",
    )(in_vmem(weight), *(in_vmem(x.reshape(tiles.shape)) for x in mine))
    sums = [x.reshape(part.shape) for x in sums]
    sums = [sums[0]] + [
        onward(sums[q], q // CORES, q % CORES) for q in range(1, PARTNERS * CORES)
    ]
    return pl.pallas_call(
        gather_kernel,
        out_shape=jax.ShapeDtypeStruct((1, 1, pairs, order, order), f32),
        in_specs=[VMEM] * (PARTNERS * CORES),
        out_specs=VMEM,
        compiler_params=limit,
        name="gather",
    )(*map(in_vmem, sums))


def solution(mesh):
    return jax.shard_map(
        on_device,
        mesh=mesh,
        in_specs=(
            P("tm", "sec", None, None),
            P("tm", "sec", None, None),
            P("sec", None),
            P("sec", None),
            P("sec"),
            P("sec", None, None, None),
            P("sec", None),
            P("sec", None, None),
            P("sec", None, None),
            P(),
            P(),
            P(),
        ),
        out_specs=P("tm", "sec", None, None, None),
        check_vma=False,
    )
```
